32 devices in a mesh: quad: 4 (over z), rows: 8 (over y, x, core).
Axes of the slice: x: 2, y: 2, z: 4, core: 2. Of those that a mesh axis runs over, the one named last changes fastest.
Arguments:
- right_sides: float32 [16, 16384], P(None, 'rows'), may hold values from -36 to 36
- jacobian_tiles: float32 [1280, 128, 128], P('rows'), may hold values from -15 to 1
- row_starts: int32 [128], P('rows'), may hold values from 0 to 1279, as said below
- tile_columns: int32 [1280], P('rows'), may hold values from 0 to 127, as said below
Outputs:
- moments: float32 [8, 4, 512, 256], P('rows', 'quad')
The draws below stay inside these ranges and needn't reach their ends.
Inputs may be any that keep to these rules, and one draw needn't show every extreme that they name: Tiles are stored by tile row in order; every tile row holds one tile or more, and its first tile is its diagonal tile. The tiles of tile rows k * 16 to (k + 1) * 16 - 1 occupy indices k * 160 to (k + 1) * 160 - 1, so row_starts[k * 16] = k * 160. `tile_columns`: A tile's column lies within 8 tile rows of its own tile row; that distance is reached.
All inputs are finite; a program needn't handle non-finite values.
Results may differ from the reference program's by a relative error of at most 0.0001.
Values sent between devices are 32-bit elements; how exact they have to be, the bound alone decides.
No kernel may reach another device: no remote copies, remote signals or barrier semaphores. Data moves between devices by JAX's collectives and lax.ppermute only.
A program may use at most 64 MiB of HBM per device.

```python
import jax
import jax.numpy as jnp
from jax import lax

TILE = 128
NRHS = 16
MOM = 8
ITERS = 2
ROW_TILES = 10
TR_DEV = 16
TILES_DEV = 160
NTR = 128
NTILES = 1280
ORDER = 16384
NSHIFT = 4
N_QUAD = 4
N_ROWS = 8


def tile_layout(key):
    groups = NTR // TR_DEV
    halo_tiles = TR_DEV // 2
    extra_tiles = TILES_DEV - TR_DEV
    key_owner, key_offset = jax.random.split(jax.random.fold_in(key, 11))
    owners = jax.random.randint(key_owner, (groups, extra_tiles), 0, TR_DEV)
    owners = owners.at[:, 0].set(TR_DEV - 1).at[:, 1].set(0)
    counts = 1 + jnp.sum((owners[:, :, None] == jnp.arange(TR_DEV)[None, None, :]).astype(jnp.int32), axis=1)
    starts = jnp.cumsum(counts, axis=1) - counts + (jnp.arange(groups) * TILES_DEV)[:, None]
    pointers = starts.reshape(NTR).astype(jnp.int32)
    indices = jnp.arange(NTILES)
    owner_row = jnp.sum((indices[:, None] >= pointers[None, :]).astype(jnp.int32), axis=1) - 1
    leading = indices == pointers[owner_row]
    offsets = jax.random.randint(key_offset, (NTILES,), -halo_tiles, halo_tiles + 1)
    local_index = indices % TILES_DEV
    offsets = jnp.where(local_index == TILES_DEV - 1, halo_tiles, offsets)
    offsets = jnp.where(local_index == 1, -halo_tiles, offsets)
    columns = jnp.clip(owner_row + offsets, 0, NTR - 1)
    columns = jnp.where(leading, owner_row, columns).astype(jnp.int32)
    return (pointers, columns, leading)


def draw_row_starts(key, part):
    return tile_layout(key)[0]


def draw_tile_columns(key, part):
    return tile_layout(key)[1]


def draw_jacobian_tiles(key, part):
    leading = tile_layout(key)[2]
    key_noise, key_diagonal = jax.random.split(jax.random.fold_in(key, 23))
    spread = 2.4 / (TILE * ROW_TILES) ** 0.5
    noise_part = jnp.clip(jax.random.normal(key_noise, (NTILES, TILE, TILE), jnp.float32), -4.0, 4.0)
    diagonal = jax.random.uniform(key_diagonal, (NTILES, TILE), jnp.float32, -14.0, -7.0)
    identity = jnp.eye(TILE, dtype=jnp.float32)
    return noise_part * spread + leading.astype(jnp.float32)[:, None, None] * identity[None, :, :] * diagonal[:, :, None]


def levels(stream_key, dims, pieces, smallest, high):
    gain, own = 1.0, jax.random.fold_in(stream_key, 6)
    for dim, parts in pieces:
        steps = jnp.exp(jax.random.uniform(jax.random.fold_in(own, dim), (parts,), jnp.float32, smallest / len(pieces), high / len(pieces)))
        gain = gain * jnp.repeat(steps, dims[dim] // parts).reshape([-1 if axis == dim else 1 for axis in range(len(dims))])
    return gain


def centred(rng, shape, scale, limit, cuts=(), kind=jnp.bfloat16):
    loudness = levels(rng, shape, cuts, -0.22, 0.18) if cuts else 1.0
    entries = jax.random.normal(rng, shape, jnp.float32) * scale * loudness
    return jnp.minimum(jnp.maximum(entries, -limit), limit).astype(kind)


def setup_inputs(seed: int = 0) -> dict:
    seeds = jax.random.split(jax.random.key(seed), 5)
    return {
        "right_sides": centred(seeds[0], (NRHS, ORDER), 6.0, 36.0, ((1, 8),), jnp.float32),
        "jacobian_tiles": draw_jacobian_tiles(jax.random.fold_in(seeds[4], 71), 0),
        "row_starts": draw_row_starts(jax.random.fold_in(seeds[4], 71), 0),
        "tile_columns": draw_tile_columns(jax.random.fold_in(seeds[4], 71), 0),
    }


contour_center = 3.0
contour_radius = 2.0
highest = lax.Precision.HIGHEST

def moment_table(phase_angle, point_count):
    powers = jnp.arange(1, MOM + 1).astype(jnp.float32)
    factor = contour_radius / point_count
    cosine = factor * jnp.cos(powers * phase_angle)
    sine_part = factor * jnp.sin(powers * phase_angle)
    pattern = jnp.stack([jnp.stack([cosine, sine_part]), jnp.stack([-sine_part, cosine])])
    identity = jnp.eye(NRHS, dtype=jnp.float32)
    coefficients = pattern[:, None, :, :, None] * identity[None, :, None, None, :]
    return coefficients.reshape(2 * NRHS, 2 * MOM * NRHS)

def halves(blocks):
    middle = blocks.shape[0] // 2
    return (blocks[:middle], blocks[middle:])

def scalar_times(blocks, real_part, imaginary):
    top_half, bottom_half = halves(blocks)
    return jnp.concatenate([real_part * top_half - imaginary * bottom_half, real_part * bottom_half + imaginary * top_half], axis=0)

def block_times(blocks, real_part, imaginary):
    top_half, bottom_half = halves(blocks)
    first_part = jnp.dot(real_part.T, top_half, precision=highest) - jnp.dot(imaginary.T, bottom_half, precision=highest)
    second_part = jnp.dot(real_part.T, bottom_half, precision=highest) + jnp.dot(imaginary.T, top_half, precision=highest)
    return jnp.concatenate([first_part, second_part], axis=0)

def projection(shadow, blocks):
    return jnp.einsum('ci,di->cd', shadow, blocks, precision=highest)

def complex_solve(image_gram, right_side):
    block_size = image_gram.shape[0]
    real_part, imaginary = (image_gram[:, :block_size], image_gram[:, block_size:])
    system = jnp.concatenate([jnp.concatenate([real_part, -imaginary], 1), jnp.concatenate([imaginary, real_part], 1)], 0)
    target = jnp.concatenate([right_side[:, :block_size], right_side[:, block_size:]], 0)
    solved = jnp.linalg.solve(system, target)
    return (solved[:block_size], solved[block_size:])

def omega_sums(second, partial_value):
    second_top, second_bottom = halves(second)
    partial_top, partial_bottom = halves(partial_value)
    numerator_real = jnp.sum(second * partial_value)
    numerator_imaginary = jnp.sum(second_top * partial_bottom - second_bottom * partial_top)
    denominator = jnp.sum(second * second)
    return (numerator_real / denominator, numerator_imaginary / denominator)

def solve_shift(right_sides, phase_angle, apply_jacobian):
    shift_real = contour_radius * jnp.cos(phase_angle)
    shift_imaginary = contour_center + contour_radius * jnp.sin(phase_angle)

    def operate(blocks):
        return scalar_times(blocks, shift_real, shift_imaginary) - apply_jacobian(blocks)
    residual = jnp.concatenate([right_sides, jnp.zeros_like(right_sides)], axis=0)
    direction = residual
    solution = jnp.zeros_like(residual)
    for iteration in range(ITERS):
        operated = operate(direction)
        image_gram = projection(right_sides, operated)
        step_alpha = complex_solve(image_gram, projection(right_sides, residual))
        partial_value = residual - block_times(operated, *step_alpha)
        second = operate(partial_value)
        omega_real, omega_imaginary = omega_sums(second, partial_value)
        solution = solution + block_times(direction, *step_alpha) + scalar_times(partial_value, omega_real, omega_imaginary)
        residual = partial_value - scalar_times(second, omega_real, omega_imaginary)
        beta_real, beta_imaginary = complex_solve(image_gram, projection(right_sides, second))
        direction = residual + block_times(direction - scalar_times(operated, omega_real, omega_imaginary), -beta_real, -beta_imaginary)
    return solution

def reference(right_sides, jacobian_tiles, row_starts, tile_columns):
    owner_row = jnp.sum((jnp.arange(NTILES)[:, None] >= row_starts[None, :]).astype(jnp.int32), axis=1) - 1

    def apply_jacobian(blocks):
        framed = blocks.reshape(blocks.shape[0], NTR, TILE)
        gathered = jnp.take(framed, tile_columns, axis=1)
        products = jnp.einsum('ctj,tij->tci', gathered, jacobian_tiles, precision=highest)
        summed = jax.ops.segment_sum(products, owner_row, num_segments=NTR)
        return jnp.moveaxis(summed, 0, 1).reshape(blocks.shape[0], ORDER)

    def one_shift(running, position):
        phase_angle = jnp.pi * (2 * position + 1).astype(jnp.float32) / NSHIFT
        solution = solve_shift(right_sides, phase_angle, apply_jacobian)
        added = jnp.einsum('qi,qo->io', solution, moment_table(phase_angle, NSHIFT), precision=highest)
        return (running + added, None)
    initial = jnp.zeros((ORDER, 2 * MOM * NRHS), jnp.float32)
    running, _ = lax.scan(one_shift, initial, jnp.arange(NSHIFT, dtype=jnp.int32))
    return running.reshape(N_ROWS, N_QUAD, ORDER // (N_ROWS * N_QUAD), 2 * MOM * NRHS)
```

```python
from functools import partial

import jax
import jax.numpy as jnp
import numpy as np
from jax import lax
from jax.experimental import pallas as pl
from jax.experimental.pallas import tpu as pltpu
from jax.sharding import PartitionSpec as P

MOM = 8
ITERS = 2
DEGREE = 2 * ITERS

contour_center = 3.0
contour_radius = 2.0
SHIFT = -7.0
CHUNK = 16
SPLIT_STEP = 16
GROUP = 4
highest = lax.Precision.HIGHEST
f32 = jnp.float32
bf16 = jnp.bfloat16


def vmem():
    return pl.BlockSpec(memory_space=pltpu.VMEM)


def smem():
    return pl.BlockSpec(memory_space=pltpu.SMEM)


def split_parts(value):
    high = value.astype(bf16)
    return high, (value - high.astype(f32)).astype(bf16)


def prepare_kernel(tile_rows, halo_tiles, tile_count, base_ref, starts_ref, columns_ref, tiles_ref,
                   split_ref, near_ref, far_ref, state):
    step = pl.program_id(0)
    per_step = tiles_ref.shape[0]
    size = tiles_ref.shape[1]

    @pl.when(step == 0)
    def _():
        state[0] = 0
        state[1] = 0
        state[2] = 0

    first = step * per_step
    origin = base_ref[0]
    row, near, far = state[0], state[1], state[2]
    for u in range(per_step):
        t = first + u
        following = starts_ref[jnp.minimum(row + 1, tile_rows - 1)] - starts_ref[0]
        row = row + ((row + 1 < tile_rows) & (t >= following)).astype(jnp.int32)
        column = columns_ref[t] - origin
        inside = ((column >= halo_tiles) & (column < halo_tiles + tile_rows)).astype(jnp.int32)
        entry = (t * 64 + column) * 32 + row
        near_ref[1 + near] = entry
        far_ref[1 + far] = entry
        near = near + inside
        far = far + (1 - inside)
    state[0] = row
    state[1] = near
    state[2] = far

    @pl.when(step == pl.num_programs(0) - 1)
    def _():
        near_ref[0] = near
        far_ref[0] = far
        padding = halo_tiles * 32 + tile_rows
        for u in range(CHUNK):
            near_ref[1 + near + u] = padding
            far_ref[1 + far + u] = padding

    high, low = split_parts(tiles_ref[...])
    split_ref[:, :size, :] = high
    split_ref[:, size:, :] = low


def prepare(tiles, row_starts, tile_columns, origin, tile_rows, halo_tiles):
    count, size = tiles.shape[0], tiles.shape[1]
    entries = 1 + count + CHUNK
    return pl.pallas_call(
        partial(prepare_kernel, tile_rows, halo_tiles, count),
        grid=(count // SPLIT_STEP,),
        in_specs=[smem(), smem(), smem(), pl.BlockSpec((SPLIT_STEP, size, size), lambda i: (i, 0, 0))],
        out_specs=[pl.BlockSpec((SPLIT_STEP, 2 * size, size), lambda i: (i, 0, 0)), smem(), smem()],
        out_shape=[
            jax.ShapeDtypeStruct((count, 2 * size, size), bf16),
            jax.ShapeDtypeStruct((entries,), jnp.int32),
            jax.ShapeDtypeStruct((entries,), jnp.int32),
        ],
        scratch_shapes=[pltpu.SMEM((3,), jnp.int32)],
        cost_estimate=pl.CostEstimate(flops=4 * tiles.size, bytes_accessed=8 * tiles.size, transcendentals=0),
        compiler_params=pltpu.CompilerParams(vmem_limit_bytes=12 << 20),
        name="prepare",
    )(origin, row_starts, tile_columns, tiles)


def multiply_listed(list_ref, split_ref, parts_ref, rows_ref, first_block):
    size = split_ref.shape[2]
    rhs = rows_ref.shape[1]
    rows_ref[...] = jnp.zeros_like(rows_ref)
    count = list_ref[0]

    def chunk(index, carry):
        total, last = carry
        products, owners = [], []
        for u in range(CHUNK):
            entry = list_ref[1 + index * CHUNK + u]
            row = entry & 31
            column = (entry >> 5) & 63
            tile = entry >> 11
            both = lax.dot_general(
                parts_ref[column - first_block], split_ref[tile], (((1,), (1,)), ((), ())),
                preferred_element_type=f32,
            )
            products.append((both[:rhs, :size] + both[rhs:, :size]) + (both[:rhs, size:] + both[rhs:, size:]))
            owners.append(row)
        for product, row in zip(products, owners):
            total = jnp.where(row == last, total, jnp.zeros_like(total)) + product
            rows_ref[row] = total
            last = row
        return total, last

    steps = lax.div(count + (CHUNK - 1), CHUNK)
    lax.fori_loop(0, steps, chunk, (jnp.zeros((rhs, size), f32), jnp.int32(-1)))


def store_parts(parts_ref, first, value, size):
    rhs = value.shape[0]
    high, low = split_parts(value)
    for b in range(value.shape[1] // size):
        parts_ref[first + b, :rhs, :] = high[:, b * size:(b + 1) * size]
        parts_ref[first + b, rhs:, :] = low[:, b * size:(b + 1) * size]


def near_kernel(tile_rows, halo_tiles, list_ref, split_ref, left_ref, right_ref, out_ref, parts_ref, rows_ref):
    size = split_ref.shape[2]
    half = tile_rows // 2
    store_parts(parts_ref, 0, left_ref[...], size)
    store_parts(parts_ref, half, right_ref[...], size)
    multiply_listed(list_ref, split_ref, parts_ref, rows_ref, halo_tiles)
    for r in range(tile_rows):
        source = left_ref if r < half else right_ref
        at = (r % half) * size
        out_ref[r] = rows_ref[r] - SHIFT * source[:, at:at + size]


def near_apply(entries, split, left, right, tile_rows, halo_tiles):
    rhs = left.shape[0]
    size = split.shape[2]
    return pl.pallas_call(
        partial(near_kernel, tile_rows, halo_tiles),
        in_specs=[smem(), vmem(), vmem(), vmem()],
        out_specs=vmem(),
        out_shape=jax.ShapeDtypeStruct((tile_rows, rhs, size), f32),
        scratch_shapes=[
            pltpu.VMEM((tile_rows, 2 * rhs, size), bf16),
            pltpu.VMEM((tile_rows + 1, rhs, size), f32),
        ],
        cost_estimate=pl.CostEstimate(flops=3 * split.size * rhs, bytes_accessed=2 * split.size, transcendentals=0),
        name="near",
    )(entries, split, left, right)


def far_rows(tile_rows, halo_tiles, list_ref, split_ref, low_ref, high_ref, parts_ref, rows_ref):
    size = split_ref.shape[2]
    store_parts(parts_ref, 0, low_ref[...], size)
    store_parts(parts_ref, halo_tiles + tile_rows, high_ref[...], size)
    multiply_listed(list_ref, split_ref, parts_ref, rows_ref, 0)


def far_kernel(tile_rows, halo_tiles, list_ref, split_ref, near_ref, low_ref, high_ref, left_ref, right_ref,
               parts_ref, rows_ref):
    size = split_ref.shape[2]
    half = tile_rows // 2
    far_rows(tile_rows, halo_tiles, list_ref, split_ref, low_ref, high_ref, parts_ref, rows_ref)
    for r in range(tile_rows):
        target = left_ref if r < half else right_ref
        at = (r % half) * size
        target[:, at:at + size] = near_ref[r] + rows_ref[r]


def far_scratch(split, rhs, tile_rows, halo_tiles):
    size = split.shape[2]
    return [
        pltpu.VMEM((tile_rows + 2 * halo_tiles, 2 * rhs, size), bf16),
        pltpu.VMEM((tile_rows + 1, rhs, size), f32),
    ]


def far_apply(entries, split, near, low, high, tile_rows, halo_tiles):
    rhs = low.shape[0]
    return pl.pallas_call(
        partial(far_kernel, tile_rows, halo_tiles),
        in_specs=[smem(), vmem(), vmem(), vmem(), vmem()],
        out_specs=[vmem(), vmem()],
        out_shape=[jax.ShapeDtypeStruct(low.shape, f32)] * 2,
        scratch_shapes=far_scratch(split, rhs, tile_rows, halo_tiles),
        cost_estimate=pl.CostEstimate(flops=split.size * rhs, bytes_accessed=split.size, transcendentals=0),
        name="far",
    )(entries, split, near, low, high)


def gram_kernel(tile_rows, halo_tiles, bases, out_rows, list_ref, part_ref, split_ref, near_ref, low_ref, high_ref,
                *refs):
    halves = refs[:2 * bases]
    gram_ref, slice_ref, parts_ref, rows_ref, whole_ref = refs[2 * bases:]
    size = split_ref.shape[2]
    rhs, half = low_ref.shape
    far_rows(tile_rows, halo_tiles, list_ref, split_ref, low_ref, high_ref, parts_ref, rows_ref)
    for i in range(bases):
        whole_ref[i * rhs:(i + 1) * rhs, :half] = halves[2 * i][...]
        whole_ref[i * rhs:(i + 1) * rhs, half:] = halves[2 * i + 1][...]
    for r in range(tile_rows):
        whole_ref[bases * rhs:, r * size:(r + 1) * size] = near_ref[r] + rows_ref[r]
    whole = whole_ref[...]
    gram_ref[...] = lax.dot_general(
        whole, whole, (((1,), (1,)), ((), ())), precision=highest, preferred_element_type=f32
    )
    at = pl.multiple_of(part_ref[0] * out_rows, 128)
    slice_ref[...] = whole_ref[:bases * rhs, pl.ds(at, out_rows)]


def gram_apply(entries, part, split, near, low, high, basis, tile_rows, halo_tiles, out_rows):
    rhs = low.shape[0]
    bases = len(basis) // 2
    width = (bases + 1) * rhs
    return pl.pallas_call(
        partial(gram_kernel, tile_rows, halo_tiles, bases, out_rows),
        in_specs=[smem(), smem()] + [vmem()] * (4 + len(basis)),
        out_specs=[vmem(), vmem()],
        out_shape=[
            jax.ShapeDtypeStruct((width, width), f32),
            jax.ShapeDtypeStruct((bases * rhs, out_rows), f32),
        ],
        scratch_shapes=far_scratch(split, rhs, tile_rows, halo_tiles)
        + [pltpu.VMEM((width, 2 * low.shape[1]), f32)],
        cost_estimate=pl.CostEstimate(flops=split.size * rhs, bytes_accessed=split.size, transcendentals=0),
        name="gram",
    )(entries, part, split, near, low, high, *basis)


def swapped(value):
    return pltpu.roll(value, value.shape[-1] // 2, 1)


def scaled(block, real, imaginary):
    return block * real + swapped(block) * imaginary


def stacked(blocks):
    return jnp.concatenate(blocks, axis=0)


def unstacked(value, rhs):
    return [value[i * rhs:(i + 1) * rhs] for i in range(value.shape[0] // rhs)]


def product(left, right):
    return jnp.dot(left, right, precision=highest, preferred_element_type=f32)


def solve_group(gram, zr, zi, rhs):
    lanes = 2 * GROUP * rhs
    half = lanes // 2
    lane = lax.broadcasted_iota(jnp.int32, (rhs, lanes), 1)
    line = lax.broadcasted_iota(jnp.int32, (rhs, lanes), 0)
    front = lane < half
    sign = jnp.where(lane[:1] < half, -1.0, 1.0).astype(f32)
    eye = (lane % rhs == line).astype(f32)
    tall_line = lax.broadcasted_iota(jnp.int32, (lanes, lanes), 0)
    tall_lane = lax.broadcasted_iota(jnp.int32, (lanes, lanes), 1)
    same_point = (tall_line % half) // rhs == (tall_lane % half) // rhs
    sums = same_point.astype(f32)

    def right_factor(block):
        turned = swapped(block) * sign
        return jnp.where(same_point, stacked([block] * GROUP + [turned] * GROUP), 0.0)

    def operator(blocks):
        out = [scaled(b, zr, zi) for b in blocks] + [jnp.zeros_like(blocks[0])]
        for i, b in enumerate(blocks):
            out[i + 1] = out[i + 1] - b
        return out

    def inverse(system):
        real = jnp.where(front, system, eye)
        imaginary = jnp.where(front, swapped(system), 0.0)
        origin = (lane % half) // rhs * rhs
        for p in range(rhs):
            column_r = jnp.take_along_axis(real, origin + p, axis=1)
            column_i = jnp.take_along_axis(imaginary, origin + p, axis=1)
            pivot_r, pivot_i = column_r[p:p + 1], column_i[p:p + 1]
            scale = 1.0 / (pivot_r * pivot_r + pivot_i * pivot_i)
            inverse_r, inverse_i = pivot_r * scale, -pivot_i * scale
            row_r, row_i = real[p:p + 1], imaginary[p:p + 1]
            lead_r = row_r * inverse_r - row_i * inverse_i
            lead_i = row_r * inverse_i + row_i * inverse_r
            here = line == p
            real = jnp.where(here, lead_r, real - (column_r * lead_r - column_i * lead_i))
            imaginary = jnp.where(here, lead_i, imaginary - (column_r * lead_i + column_i * lead_r))
        return jnp.where(front, swapped(real), imaginary)

    shadow = gram[:rhs]
    identity = jnp.where(front, eye, 0.0)
    direction, residual, result = [identity], [identity], []
    for iteration in range(ITERS):
        image = operator(direction)
        tall = stacked(image)
        image_gram = product(shadow[:, :tall.shape[0]], tall)
        tall_residual = stacked(residual)
        residual_gram = product(shadow[:, :tall_residual.shape[0]], tall_residual)
        solver = inverse(image_gram)
        alpha = right_factor(product(solver, right_factor(residual_gram)))
        moved = unstacked(product(stacked(image + direction), alpha), rhs)
        moved_image, moved_direction = moved[:len(image)], moved[len(image):]
        partial_block = [-m for m in moved_image]
        for i, r in enumerate(residual):
            partial_block[i] = partial_block[i] + r
        second = operator(partial_block)
        tall_second = stacked(second)
        tall_partial = stacked(partial_block + [jnp.zeros_like(identity)])
        depth = tall_second.shape[0]
        weighted = product(gram[:depth, :depth], tall_second)
        turned = swapped(weighted) * -sign
        lines = [
            jnp.sum(tall_second * weighted, axis=0, keepdims=True),
            jnp.sum(tall_partial * weighted, axis=0, keepdims=True),
            jnp.sum(tall_partial * turned, axis=0, keepdims=True),
        ]
        spread = product(stacked(lines + [jnp.zeros((5, lanes), f32)]), sums)
        inverse_norm = 1.0 / spread[0:1]
        omega_r = spread[1:2] * inverse_norm
        omega_i = -spread[2:3] * inverse_norm * sign
        step = [scaled(b, omega_r, omega_i) for b in partial_block]
        for i, m in enumerate(moved_direction):
            step[i] = step[i] + m
        for i, r in enumerate(result):
            step[i] = step[i] + r
        result = step
        if iteration + 1 < ITERS:
            residual = [-scaled(b, omega_r, omega_i) for b in second]
            for i, s in enumerate(partial_block):
                residual[i] = residual[i] + s
            beta = -product(solver, right_factor(weighted[:rhs]))
            base = [-scaled(b, omega_r, omega_i) for b in image]
            for i, d in enumerate(direction):
                base[i] = base[i] + d
            turned_base = unstacked(product(stacked(base), right_factor(beta)), rhs)
            direction = list(residual)
            for i, b in enumerate(turned_base):
                direction[i] = direction[i] + b
    return stacked(result)


def finish_kernel(rhs, groups, grams, *refs):
    gram_refs, (points_ref, table_ref, slice_ref, out_ref) = refs[:grams], refs[grams:]
    gram = gram_refs[0][...]
    for ref in gram_refs[1:]:
        gram = gram + ref[...]
    lanes = 2 * GROUP * rhs
    weights = None
    for g in range(groups):
        solved = solve_group(gram, points_ref[2 * g:2 * g + 1], points_ref[2 * g + 1:2 * g + 2], rhs)
        term = product(solved, table_ref[g * lanes:(g + 1) * lanes])
        weights = term if weights is None else weights + term
    out_ref[...] = lax.dot_general(
        slice_ref[...], weights, (((0,), (0,)), ((), ())), precision=highest, preferred_element_type=f32
    )


def contour_tables(point_count, rhs):
    groups = -(-point_count // GROUP)
    points = np.zeros((-(-2 * groups // 8) * 8, 2 * GROUP * rhs), np.float32)
    table = np.zeros((groups, 2, GROUP, rhs, 2, MOM, rhs), np.float32)
    factor = contour_radius / point_count
    powers = np.arange(1, MOM + 1)
    for j in range(groups * GROUP):
        g, slot = divmod(j, GROUP)
        angle = np.pi * (2 * min(j, point_count - 1) + 1) / point_count
        lanes = np.arange(slot * rhs, (slot + 1) * rhs)
        points[2 * g, lanes] = points[2 * g, GROUP * rhs + lanes] = contour_radius * np.cos(angle) - SHIFT
        imaginary = contour_center + contour_radius * np.sin(angle)
        points[2 * g + 1, lanes] = -imaginary
        points[2 * g + 1, GROUP * rhs + lanes] = imaginary
        if j >= point_count:
            continue
        cosine, sine = factor * np.cos(powers * angle), factor * np.sin(powers * angle)
        for c in range(rhs):
            table[g, 0, slot, c, 0, :, c] = cosine
            table[g, 0, slot, c, 1, :, c] = sine
            table[g, 1, slot, c, 0, :, c] = -sine
            table[g, 1, slot, c, 1, :, c] = cosine
    return groups, points, table.reshape(groups * 2 * GROUP * rhs, 2 * MOM * rhs)


def finish(grams, basis_slice, point_count, rhs):
    groups, points, table = contour_tables(point_count, rhs)
    return pl.pallas_call(
        partial(finish_kernel, rhs, groups, len(grams)),
        in_specs=[vmem()] * (len(grams) + 3),
        out_specs=vmem(),
        out_shape=jax.ShapeDtypeStruct((basis_slice.shape[1], table.shape[1]), f32),
        name="finish",
    )(*grams, jnp.asarray(points), jnp.asarray(table), basis_slice)


def body(right_sides, jacobian_tiles, row_starts, tile_columns):
    tile_rows = row_starts.shape[0]
    rhs = right_sides.shape[0]
    halo_tiles = tile_rows // 2
    half = right_sides.shape[1] // 2
    count = lax.axis_size("rows")
    quad_count = lax.axis_size("quad")
    forward = [(i, (i + 1) % count) for i in range(count)]
    backward = [(target, source) for source, target in forward]
    origin = (lax.axis_index("rows") * tile_rows - halo_tiles).reshape(1)
    part = lax.axis_index("quad").reshape(1)
    out_rows = right_sides.shape[1] // quad_count

    left, right = right_sides[:, :half], right_sides[:, half:]
    low = lax.ppermute(right, "rows", forward)
    high = lax.ppermute(left, "rows", backward)
    split, near_list, far_list = prepare(jacobian_tiles, row_starts, tile_columns, origin, tile_rows, halo_tiles)
    basis = []
    for power in range(DEGREE):
        if power > 0:
            low = lax.ppermute(right, "rows", forward)
            high = lax.ppermute(left, "rows", backward)
        basis += [left, right]
        near = near_apply(near_list, split, left, right, tile_rows, halo_tiles)
        if power + 1 < DEGREE:
            left, right = far_apply(far_list, split, near, low, high, tile_rows, halo_tiles)
    gram, basis_slice = gram_apply(
        far_list, part, split, near, low, high, basis, tile_rows, halo_tiles, out_rows
    )
    distance = 1
    while distance * 4 < count:
        gram = gram + lax.ppermute(gram, "rows", [(i, i ^ distance) for i in range(count)])
        distance *= 2
    grams = [gram] + [
        lax.ppermute(gram, "rows", [(i, i ^ (distance * k)) for i in range(count)])
        for k in range(1, count // distance)
    ]
    result = finish(grams, basis_slice, quad_count, rhs)
    return result.reshape(1, 1, result.shape[0], result.shape[1])


def solution(mesh):
    in_specs = (P(None, "rows"), P("rows", None, None), P("rows"), P("rows"))
    out_specs = P("rows", "quad", None, None)
    return jax.shard_map(body, mesh=mesh, in_specs=in_specs, out_specs=out_specs, check_vma=False)
```

```python
from functools import partial

import jax
import jax.numpy as jnp
import numpy as np
from jax import lax
from jax.experimental import pallas as pl
from jax.experimental.pallas import tpu as pltpu
from jax.sharding import PartitionSpec as P

MOM = 8
ITERS = 2
DEGREE = 2 * ITERS

contour_center = 3.0
contour_radius = 2.0
SHIFT = -7.0
CHUNK = 16
SPLIT_STEP = 16
KERNEL_VMEM = 16 << 20
GROUP = 4
highest = lax.Precision.HIGHEST
f32 = jnp.float32
bf16 = jnp.bfloat16


def vmem():
    return pl.BlockSpec(memory_space=pltpu.VMEM)


def smem():
    return pl.BlockSpec(memory_space=pltpu.SMEM)


def split_parts(value):
    high = value.astype(bf16)
    return high, (value - high.astype(f32)).astype(bf16)


def prepare_kernel(tile_rows, halo_tiles, quad_count, base_ref, starts_ref, columns_ref, tiles_ref,
                   split_ref, near_ref, far_ref, state):
    step = pl.program_id(0)
    per_step = tiles_ref.shape[0]
    size = tiles_ref.shape[1]

    @pl.when(step == 0)
    def _():
        state[0] = 0
        state[1] = 0
        state[2] = 0

    first = step * per_step
    origin = lax.div(base_ref[0], quad_count) * tile_rows - halo_tiles
    row, near, far = state[0], state[1], state[2]
    for u in range(per_step):
        t = first + u
        following = starts_ref[jnp.minimum(row + 1, tile_rows - 1)] - starts_ref[0]
        row = row + ((row + 1 < tile_rows) & (t >= following)).astype(jnp.int32)
        column = columns_ref[t] - origin
        inside = ((column >= halo_tiles) & (column < halo_tiles + tile_rows)).astype(jnp.int32)
        entry = (t * 64 + column) * 32 + row
        near_ref[1 + near] = entry
        far_ref[1 + far] = entry
        near = near + inside
        far = far + (1 - inside)
    state[0] = row
    state[1] = near
    state[2] = far

    @pl.when(step == pl.num_programs(0) - 1)
    def _():
        near_ref[0] = near
        far_ref[0] = far
        padding = halo_tiles * 32 + tile_rows
        for u in range(CHUNK):
            near_ref[1 + near + u] = padding
            far_ref[1 + far + u] = padding

    high, low = split_parts(tiles_ref[...])
    split_ref[:, :size, :] = high
    split_ref[:, size:, :] = low


def prepare(tiles, row_starts, tile_columns, place, quad_count, tile_rows, halo_tiles):
    count, size = tiles.shape[0], tiles.shape[1]
    entries = 1 + count + CHUNK
    return pl.pallas_call(
        partial(prepare_kernel, tile_rows, halo_tiles, quad_count),
        grid=(count // SPLIT_STEP,),
        in_specs=[smem(), smem(), smem(), pl.BlockSpec((SPLIT_STEP, size, size), lambda i: (i, 0, 0))],
        out_specs=[pl.BlockSpec((SPLIT_STEP, 2 * size, size), lambda i: (i, 0, 0)), smem(), smem()],
        out_shape=[
            jax.ShapeDtypeStruct((count, 2 * size, size), bf16),
            jax.ShapeDtypeStruct((entries,), jnp.int32),
            jax.ShapeDtypeStruct((entries,), jnp.int32),
        ],
        scratch_shapes=[pltpu.SMEM((3,), jnp.int32)],
        cost_estimate=pl.CostEstimate(flops=4 * tiles.size, bytes_accessed=8 * tiles.size, transcendentals=0),
        compiler_params=pltpu.CompilerParams(vmem_limit_bytes=12 << 20),
        name="prepare",
    )(place, row_starts, tile_columns, pltpu.with_memory_space_constraint(tiles, pltpu.HBM))


def multiply_listed(list_ref, split_ref, parts_ref, rows_ref, first_block):
    size = split_ref.shape[2]
    rhs = rows_ref.shape[1]
    rows_ref[...] = jnp.zeros_like(rows_ref)
    count = list_ref[0]

    def chunk(index, carry):
        total, last = carry
        products, owners = [], []
        for u in range(CHUNK):
            entry = list_ref[1 + index * CHUNK + u]
            row = entry & 31
            column = (entry >> 5) & 63
            tile = entry >> 11
            both = lax.dot_general(
                parts_ref[column - first_block], split_ref[tile], (((1,), (1,)), ((), ())),
                preferred_element_type=f32,
            )
            products.append((both[:rhs, :size] + both[rhs:, :size]) + (both[:rhs, size:] + both[rhs:, size:]))
            owners.append(row)
        for product, row in zip(products, owners):
            total = jnp.where(row == last, total, jnp.zeros_like(total)) + product
            rows_ref[row] = total
            last = row
        return total, last

    steps = lax.div(count + (CHUNK - 1), CHUNK)
    lax.fori_loop(0, steps, chunk, (jnp.zeros((rhs, size), f32), jnp.int32(-1)))


def store_parts(parts_ref, first, value, size):
    rhs = value.shape[0]
    high, low = split_parts(value)
    for b in range(value.shape[1] // size):
        parts_ref[first + b, :rhs, :] = high[:, b * size:(b + 1) * size]
        parts_ref[first + b, rhs:, :] = low[:, b * size:(b + 1) * size]


def near_kernel(tile_rows, halo_tiles, list_ref, split_ref, left_ref, right_ref, out_ref, parts_ref, rows_ref):
    size = split_ref.shape[2]
    half = tile_rows // 2
    store_parts(parts_ref, 0, left_ref[...], size)
    store_parts(parts_ref, half, right_ref[...], size)
    multiply_listed(list_ref, split_ref, parts_ref, rows_ref, halo_tiles)
    for r in range(tile_rows):
        source = left_ref if r < half else right_ref
        at = (r % half) * size
        out_ref[r] = rows_ref[r] - SHIFT * source[:, at:at + size]


def near_apply(entries, split, left, right, tile_rows, halo_tiles):
    rhs = left.shape[0]
    size = split.shape[2]
    return pl.pallas_call(
        partial(near_kernel, tile_rows, halo_tiles),
        in_specs=[smem(), vmem(), vmem(), vmem()],
        out_specs=vmem(),
        out_shape=jax.ShapeDtypeStruct((tile_rows, rhs, size), f32),
        scratch_shapes=[
            pltpu.VMEM((tile_rows, 2 * rhs, size), bf16),
            pltpu.VMEM((tile_rows + 1, rhs, size), f32),
        ],
        cost_estimate=pl.CostEstimate(flops=3 * split.size * rhs, bytes_accessed=2 * split.size, transcendentals=0),
        compiler_params=pltpu.CompilerParams(vmem_limit_bytes=KERNEL_VMEM),
        name="near",
    )(entries, split, left, right)


def far_rows(tile_rows, halo_tiles, list_ref, split_ref, low_ref, high_ref, parts_ref, rows_ref):
    size = split_ref.shape[2]
    store_parts(parts_ref, 0, low_ref[...], size)
    store_parts(parts_ref, halo_tiles + tile_rows, high_ref[...], size)
    multiply_listed(list_ref, split_ref, parts_ref, rows_ref, 0)


def far_kernel(tile_rows, halo_tiles, list_ref, split_ref, near_ref, low_ref, high_ref, left_ref, right_ref,
               parts_ref, rows_ref):
    size = split_ref.shape[2]
    half = tile_rows // 2
    far_rows(tile_rows, halo_tiles, list_ref, split_ref, low_ref, high_ref, parts_ref, rows_ref)
    for r in range(tile_rows):
        target = left_ref if r < half else right_ref
        at = (r % half) * size
        target[:, at:at + size] = near_ref[r] + rows_ref[r]


def far_scratch(split, rhs, tile_rows, halo_tiles):
    size = split.shape[2]
    return [
        pltpu.VMEM((tile_rows + 2 * halo_tiles, 2 * rhs, size), bf16),
        pltpu.VMEM((tile_rows + 1, rhs, size), f32),
    ]


def far_apply(entries, split, near, low, high, tile_rows, halo_tiles):
    rhs = low.shape[0]
    return pl.pallas_call(
        partial(far_kernel, tile_rows, halo_tiles),
        in_specs=[smem(), vmem(), vmem(), vmem(), vmem()],
        out_specs=[vmem(), vmem()],
        out_shape=[jax.ShapeDtypeStruct(low.shape, f32)] * 2,
        scratch_shapes=far_scratch(split, rhs, tile_rows, halo_tiles),
        cost_estimate=pl.CostEstimate(flops=split.size * rhs, bytes_accessed=split.size, transcendentals=0),
        compiler_params=pltpu.CompilerParams(vmem_limit_bytes=KERNEL_VMEM),
        name="far",
    )(entries, split, near, low, high)


def gram_kernel(tile_rows, halo_tiles, bases, out_rows, list_ref, place_ref, split_ref, near_ref, low_ref, high_ref,
                *refs):
    halves = refs[:2 * bases]
    gram_ref, slice_ref, parts_ref, rows_ref, whole_ref = refs[2 * bases:]
    size = split_ref.shape[2]
    rhs, half = low_ref.shape
    far_rows(tile_rows, halo_tiles, list_ref, split_ref, low_ref, high_ref, parts_ref, rows_ref)
    for i in range(bases):
        whole_ref[i * rhs:(i + 1) * rhs, :half] = halves[2 * i][...]
        whole_ref[i * rhs:(i + 1) * rhs, half:] = halves[2 * i + 1][...]
    for r in range(tile_rows):
        whole_ref[bases * rhs:, r * size:(r + 1) * size] = near_ref[r] + rows_ref[r]
    whole = whole_ref[...]
    gram_ref[...] = lax.dot_general(
        whole, whole, (((1,), (1,)), ((), ())), precision=highest, preferred_element_type=f32
    )
    at = pl.multiple_of(lax.rem(place_ref[0], whole.shape[1] // out_rows) * out_rows, 128)
    slice_ref[...] = whole_ref[:bases * rhs, pl.ds(at, out_rows)]


def gram_apply(entries, place, split, near, low, high, basis, tile_rows, halo_tiles, out_rows):
    rhs = low.shape[0]
    bases = len(basis) // 2
    width = (bases + 1) * rhs
    return pl.pallas_call(
        partial(gram_kernel, tile_rows, halo_tiles, bases, out_rows),
        in_specs=[smem(), smem()] + [vmem()] * (4 + len(basis)),
        out_specs=[vmem(), vmem()],
        out_shape=[
            jax.ShapeDtypeStruct((width, width), f32),
            jax.ShapeDtypeStruct((bases * rhs, out_rows), f32),
        ],
        scratch_shapes=far_scratch(split, rhs, tile_rows, halo_tiles)
        + [pltpu.VMEM((width, 2 * low.shape[1]), f32)],
        cost_estimate=pl.CostEstimate(flops=split.size * rhs, bytes_accessed=split.size, transcendentals=0),
        compiler_params=pltpu.CompilerParams(vmem_limit_bytes=KERNEL_VMEM),
        name="gram",
    )(entries, place, split, near, low, high, *basis)


def swapped(value):
    return pltpu.roll(value, value.shape[-1] // 2, 1)


def scaled(block, real, imaginary):
    return block * real + swapped(block) * imaginary


def stacked(blocks):
    return jnp.concatenate(blocks, axis=0)


def unstacked(value, rhs):
    return [value[i * rhs:(i + 1) * rhs] for i in range(value.shape[0] // rhs)]


def product(left, right):
    return jnp.dot(left, right, precision=highest, preferred_element_type=f32)


def solve_group(gram, zr, zi, rhs):
    lanes = 2 * GROUP * rhs
    half = lanes // 2
    lane = lax.broadcasted_iota(jnp.int32, (rhs, lanes), 1)
    line = lax.broadcasted_iota(jnp.int32, (rhs, lanes), 0)
    front = lane < half
    sign = jnp.where(lane[:1] < half, -1.0, 1.0).astype(f32)
    eye = (lane % rhs == line).astype(f32)
    tall_line = lax.broadcasted_iota(jnp.int32, (lanes, lanes), 0)
    tall_lane = lax.broadcasted_iota(jnp.int32, (lanes, lanes), 1)
    same_point = (tall_line % half) // rhs == (tall_lane % half) // rhs
    sums = same_point.astype(f32)

    def right_factor(block):
        turned = swapped(block) * sign
        return jnp.where(same_point, stacked([block] * GROUP + [turned] * GROUP), 0.0)

    def operator(blocks):
        out = [scaled(b, zr, zi) for b in blocks] + [jnp.zeros_like(blocks[0])]
        for i, b in enumerate(blocks):
            out[i + 1] = out[i + 1] - b
        return out

    def inverse(system):
        real = jnp.where(front, system, eye)
        imaginary = jnp.where(front, swapped(system), 0.0)
        origin = (lane % half) // rhs * rhs
        for p in range(rhs):
            column_r = jnp.take_along_axis(real, origin + p, axis=1)
            column_i = jnp.take_along_axis(imaginary, origin + p, axis=1)
            pivot_r, pivot_i = column_r[p:p + 1], column_i[p:p + 1]
            scale = 1.0 / (pivot_r * pivot_r + pivot_i * pivot_i)
            inverse_r, inverse_i = pivot_r * scale, -pivot_i * scale
            row_r, row_i = real[p:p + 1], imaginary[p:p + 1]
            lead_r = row_r * inverse_r - row_i * inverse_i
            lead_i = row_r * inverse_i + row_i * inverse_r
            here = line == p
            real = jnp.where(here, lead_r, real - (column_r * lead_r - column_i * lead_i))
            imaginary = jnp.where(here, lead_i, imaginary - (column_r * lead_i + column_i * lead_r))
        return jnp.where(front, swapped(real), imaginary)

    shadow = gram[:rhs]
    identity = jnp.where(front, eye, 0.0)
    direction, residual, result = [identity], [identity], []
    for iteration in range(ITERS):
        image = operator(direction)
        tall = stacked(image)
        image_gram = product(shadow[:, :tall.shape[0]], tall)
        tall_residual = stacked(residual)
        residual_gram = product(shadow[:, :tall_residual.shape[0]], tall_residual)
        solver = inverse(image_gram)
        alpha = right_factor(product(solver, right_factor(residual_gram)))
        moved = unstacked(product(stacked(image + direction), alpha), rhs)
        moved_image, moved_direction = moved[:len(image)], moved[len(image):]
        partial_block = [-m for m in moved_image]
        for i, r in enumerate(residual):
            partial_block[i] = partial_block[i] + r
        second = operator(partial_block)
        tall_second = stacked(second)
        tall_partial = stacked(partial_block + [jnp.zeros_like(identity)])
        depth = tall_second.shape[0]
        weighted = product(gram[:depth, :depth], tall_second)
        turned = swapped(weighted) * -sign
        lines = [
            jnp.sum(tall_second * weighted, axis=0, keepdims=True),
            jnp.sum(tall_partial * weighted, axis=0, keepdims=True),
            jnp.sum(tall_partial * turned, axis=0, keepdims=True),
        ]
        spread = product(stacked(lines + [jnp.zeros((5, lanes), f32)]), sums)
        inverse_norm = 1.0 / spread[0:1]
        omega_r = spread[1:2] * inverse_norm
        omega_i = -spread[2:3] * inverse_norm * sign
        step = [scaled(b, omega_r, omega_i) for b in partial_block]
        for i, m in enumerate(moved_direction):
            step[i] = step[i] + m
        for i, r in enumerate(result):
            step[i] = step[i] + r
        result = step
        if iteration + 1 < ITERS:
            residual = [-scaled(b, omega_r, omega_i) for b in second]
            for i, s in enumerate(partial_block):
                residual[i] = residual[i] + s
            beta = -product(solver, right_factor(weighted[:rhs]))
            base = [-scaled(b, omega_r, omega_i) for b in image]
            for i, d in enumerate(direction):
                base[i] = base[i] + d
            turned_base = unstacked(product(stacked(base), right_factor(beta)), rhs)
            direction = list(residual)
            for i, b in enumerate(turned_base):
                direction[i] = direction[i] + b
    return stacked(result)


def finish_kernel(rhs, groups, grams, *refs):
    gram_refs, (points_ref, table_ref, slice_ref, out_ref) = refs[:grams], refs[grams:]
    gram = gram_refs[0][...]
    for ref in gram_refs[1:]:
        gram = gram + ref[...]
    lanes = 2 * GROUP * rhs
    weights = None
    for g in range(groups):
        solved = solve_group(gram, points_ref[2 * g:2 * g + 1], points_ref[2 * g + 1:2 * g + 2], rhs)
        term = product(solved, table_ref[g * lanes:(g + 1) * lanes])
        weights = term if weights is None else weights + term
    out_ref[...] = lax.dot_general(
        slice_ref[...], weights, (((0,), (0,)), ((), ())), precision=highest, preferred_element_type=f32
    )


def contour_tables(point_count, rhs):
    groups = -(-point_count // GROUP)
    points = np.zeros((-(-2 * groups // 8) * 8, 2 * GROUP * rhs), np.float32)
    table = np.zeros((groups, 2, GROUP, rhs, 2, MOM, rhs), np.float32)
    factor = contour_radius / point_count
    powers = np.arange(1, MOM + 1)
    for j in range(groups * GROUP):
        g, slot = divmod(j, GROUP)
        angle = np.pi * (2 * min(j, point_count - 1) + 1) / point_count
        lanes = np.arange(slot * rhs, (slot + 1) * rhs)
        points[2 * g, lanes] = points[2 * g, GROUP * rhs + lanes] = contour_radius * np.cos(angle) - SHIFT
        imaginary = contour_center + contour_radius * np.sin(angle)
        points[2 * g + 1, lanes] = -imaginary
        points[2 * g + 1, GROUP * rhs + lanes] = imaginary
        if j >= point_count:
            continue
        cosine, sine = factor * np.cos(powers * angle), factor * np.sin(powers * angle)
        for c in range(rhs):
            table[g, 0, slot, c, 0, :, c] = cosine
            table[g, 0, slot, c, 1, :, c] = sine
            table[g, 1, slot, c, 0, :, c] = -sine
            table[g, 1, slot, c, 1, :, c] = cosine
    return groups, points, table.reshape(groups * 2 * GROUP * rhs, 2 * MOM * rhs)


def finish(grams, basis_slice, point_count, rhs):
    groups, points, table = contour_tables(point_count, rhs)
    return pl.pallas_call(
        partial(finish_kernel, rhs, groups, len(grams)),
        in_specs=[vmem()] * (len(grams) + 3),
        out_specs=vmem(),
        out_shape=jax.ShapeDtypeStruct((basis_slice.shape[1], table.shape[1]), f32),
        compiler_params=pltpu.CompilerParams(vmem_limit_bytes=KERNEL_VMEM),
        name="finish",
    )(*grams, jnp.asarray(points), jnp.asarray(table), basis_slice)


def body(right_sides, jacobian_tiles, row_starts, tile_columns):
    tile_rows = row_starts.shape[0]
    rhs = right_sides.shape[0]
    halo_tiles = tile_rows // 2
    half = right_sides.shape[1] // 2
    count = lax.axis_size("rows")
    quad_count = lax.axis_size("quad")
    forward = [(i, (i + 1) % count) for i in range(count)]
    backward = [(target, source) for source, target in forward]
    place = (lax.axis_index("rows") * quad_count + lax.axis_index("quad")).reshape(1)
    out_rows = right_sides.shape[1] // quad_count

    left, right = right_sides[:, :half], right_sides[:, half:]
    low = lax.ppermute(right, "rows", forward)
    high = lax.ppermute(left, "rows", backward)
    split, near_list, far_list = prepare(jacobian_tiles, row_starts, tile_columns, place, quad_count, tile_rows, halo_tiles)
    basis = []
    for power in range(DEGREE):
        if power > 0:
            low = lax.ppermute(right, "rows", forward)
            high = lax.ppermute(left, "rows", backward)
        basis += [left, right]
        near = near_apply(near_list, split, left, right, tile_rows, halo_tiles)
        if power + 1 < DEGREE:
            left, right = far_apply(far_list, split, near, low, high, tile_rows, halo_tiles)
    gram, basis_slice = gram_apply(
        far_list, place, split, near, low, high, basis, tile_rows, halo_tiles, out_rows
    )
    distance = 1
    while distance * 4 < count:
        gram = gram + lax.ppermute(gram, "rows", [(i, i ^ distance) for i in range(count)])
        distance *= 2
    grams = [gram] + [
        lax.ppermute(gram, "rows", [(i, i ^ (distance * k)) for i in range(count)])
        for k in range(1, count // distance)
    ]
    result = finish(grams, basis_slice, quad_count, rhs)
    return result.reshape(1, 1, result.shape[0], result.shape[1])


def solution(mesh):
    in_specs = (P(None, "rows"), P("rows", None, None), P("rows"), P("rows"))
    out_specs = P("rows", "quad", None, None)
    return jax.shard_map(body, mesh=mesh, in_specs=in_specs, out_specs=out_specs, check_vma=False)
```

```python
from functools import partial

import jax
import jax.numpy as jnp
import numpy as np
from jax import lax
from jax.experimental import pallas as pl
from jax.experimental.pallas import tpu as pltpu
from jax.sharding import PartitionSpec as P

MOM = 8
ITERS = 2
DEGREE = 2 * ITERS

contour_center = 3.0
contour_radius = 2.0
SHIFT = -7.0
CHUNK = 32
SPLIT_STEP = 16
KERNEL_VMEM = 16 << 20
GROUP = 4
highest = lax.Precision.HIGHEST
f32 = jnp.float32
bf16 = jnp.bfloat16


def vmem():
    return pl.BlockSpec(memory_space=pltpu.VMEM)


def smem():
    return pl.BlockSpec(memory_space=pltpu.SMEM)


def split_parts(value):
    high = value.astype(bf16)
    return high, (value - high.astype(f32)).astype(bf16)


def first_kernel(tile_rows, halo_tiles, quad_count, place_ref, starts_hbm, columns_hbm, tiles_hbm, left_ref, right_ref,
                 split_ref, near_ref, far_ref, out_ref, tiles_ref, parts_ref, rows_ref, starts_ref, columns_ref,
                 tile_sems, index_sems):
    count, size = tiles_ref.shape[0], tiles_ref.shape[1]
    rhs = left_ref.shape[0]
    half = tile_rows // 2
    starts_copy = pltpu.make_async_copy(starts_hbm, starts_ref, index_sems.at[0])
    columns_copy = pltpu.make_async_copy(columns_hbm, columns_ref, index_sems.at[1])
    starts_copy.start()
    columns_copy.start()

    def tiles_copy(step):
        span = pl.ds(step * SPLIT_STEP, SPLIT_STEP)
        return pltpu.make_async_copy(tiles_hbm.at[span], tiles_ref.at[span], tile_sems.at[step])

    for step in range(count // SPLIT_STEP):
        tiles_copy(step).start()
    store_parts(parts_ref, 0, left_ref[...], size)
    store_parts(parts_ref, half, right_ref[...], size)
    starts_copy.wait()
    columns_copy.wait()
    origin = lax.div(place_ref[0], quad_count) * tile_rows - halo_tiles
    base = starts_ref[0]

    def chunk(step, carry):
        row, near, far, total = carry
        tiles_copy(step).wait()
        for u in range(SPLIT_STEP):
            t = step * SPLIT_STEP + u
            following = starts_ref[jnp.minimum(row + 1, tile_rows - 1)] - base
            fresh = (row + 1 < tile_rows) & (t >= following)
            row = row + fresh.astype(jnp.int32)
            column = columns_ref[t] - origin
            inside = (column >= halo_tiles) & (column < halo_tiles + tile_rows)
            entry = (t * 64 + column) * 32 + row
            near_ref[1 + near] = entry
            far_ref[1 + far] = entry
            counted = inside.astype(jnp.int32)
            near = near + counted
            far = far + (1 - counted)
            high, low = split_parts(tiles_ref[t].T)
            split_ref[t, :, :size] = high
            split_ref[t, :, size:] = low
            local = jnp.clip(column - halo_tiles, 0, tile_rows - 1)
            both = jnp.dot(parts_ref[local], jnp.concatenate([high, low], axis=1), preferred_element_type=f32)
            term = (both[:rhs, :size] + both[rhs:, :size]) + (both[:rhs, size:] + both[rhs:, size:])
            zero = jnp.zeros_like(total)
            total = jnp.where(fresh, zero, total) + jnp.where(inside, term, zero)
            rows_ref[row] = total
        return row, near, far, total

    zero = jnp.int32(0)
    _, near, far, _ = lax.fori_loop(
        0, count // SPLIT_STEP, chunk, (zero, zero, zero, jnp.zeros((rhs, size), f32))
    )
    near_ref[0] = near
    far_ref[0] = far
    padding = halo_tiles * 32 + tile_rows
    for u in range(CHUNK):
        near_ref[1 + near + u] = padding
        far_ref[1 + far + u] = padding
    shifted_rows(tile_rows, rows_ref, left_ref, right_ref, out_ref)


def shifted_rows(tile_rows, rows_ref, left_ref, right_ref, out_ref):
    half = tile_rows // 2
    size = rows_ref.shape[2]
    for r in range(tile_rows):
        source = left_ref if r < half else right_ref
        at = (r % half) * size
        out_ref[r] = rows_ref[r] - SHIFT * source[:, at:at + size]


def first_apply(tiles, row_starts, tile_columns, place, left, right, quad_count, tile_rows, halo_tiles):
    count, size = tiles.shape[0], tiles.shape[1]
    rhs = left.shape[0]
    entries = 1 + count + CHUNK
    hbm = pl.BlockSpec(memory_space=pl.ANY)
    return pl.pallas_call(
        partial(first_kernel, tile_rows, halo_tiles, quad_count),
        in_specs=[smem(), hbm, hbm, hbm, vmem(), vmem()],
        out_specs=[vmem(), smem(), smem(), vmem()],
        out_shape=[
            jax.ShapeDtypeStruct((count, size, 2 * size), bf16),
            jax.ShapeDtypeStruct((entries,), jnp.int32),
            jax.ShapeDtypeStruct((entries,), jnp.int32),
            jax.ShapeDtypeStruct((tile_rows, rhs, size), f32),
        ],
        scratch_shapes=[
            pltpu.VMEM((count, size, size), f32),
            pltpu.VMEM((tile_rows, 2 * rhs, size), bf16),
            pltpu.VMEM((tile_rows, rhs, size), f32),
            pltpu.SMEM((tile_rows,), jnp.int32),
            pltpu.SMEM((count,), jnp.int32),
            pltpu.SemaphoreType.DMA((count // SPLIT_STEP,)),
            pltpu.SemaphoreType.DMA((2,)),
        ],
        cost_estimate=pl.CostEstimate(flops=8 * tiles.size * rhs, bytes_accessed=8 * tiles.size, transcendentals=0),
        compiler_params=pltpu.CompilerParams(vmem_limit_bytes=24 << 20),
        name="first",
    )(
        place,
        pltpu.with_memory_space_constraint(row_starts, pltpu.HBM),
        pltpu.with_memory_space_constraint(tile_columns, pltpu.HBM),
        pltpu.with_memory_space_constraint(tiles, pltpu.HBM),
        left,
        right,
    )


def multiply_listed(list_ref, split_ref, parts_ref, rows_ref, first_block):
    rhs, size = rows_ref.shape[1:]
    rows_ref[...] = jnp.zeros_like(rows_ref)
    count = list_ref[0]

    def chunk(index, carry):
        total, last = carry
        products, owners = [], []
        for u in range(CHUNK):
            entry = list_ref[1 + index * CHUNK + u]
            row = entry & 31
            column = (entry >> 5) & 63
            tile = entry >> 11
            both = jnp.dot(parts_ref[column - first_block], split_ref[tile], preferred_element_type=f32)
            products.append((both[:rhs, :size] + both[rhs:, :size]) + (both[:rhs, size:] + both[rhs:, size:]))
            owners.append(row)
        for product, row in zip(products, owners):
            total = jnp.where(row == last, total, jnp.zeros_like(total)) + product
            rows_ref[row] = total
            last = row
        return total, last

    steps = lax.div(count + (CHUNK - 1), CHUNK)
    lax.fori_loop(0, steps, chunk, (jnp.zeros((rhs, size), f32), jnp.int32(-1)))


def store_parts(parts_ref, first, value, size):
    rhs = value.shape[0]
    high, low = split_parts(value)
    for b in range(value.shape[1] // size):
        parts_ref[first + b, :rhs, :] = high[:, b * size:(b + 1) * size]
        parts_ref[first + b, rhs:, :] = low[:, b * size:(b + 1) * size]


def near_kernel(tile_rows, halo_tiles, list_ref, split_ref, left_ref, right_ref, out_ref, parts_ref, rows_ref):
    size = split_ref.shape[1]
    half = tile_rows // 2
    store_parts(parts_ref, 0, left_ref[...], size)
    store_parts(parts_ref, half, right_ref[...], size)
    multiply_listed(list_ref, split_ref, parts_ref, rows_ref, halo_tiles)
    shifted_rows(tile_rows, rows_ref, left_ref, right_ref, out_ref)


def near_apply(entries, split, left, right, tile_rows, halo_tiles):
    rhs = left.shape[0]
    size = split.shape[1]
    return pl.pallas_call(
        partial(near_kernel, tile_rows, halo_tiles),
        in_specs=[smem(), vmem(), vmem(), vmem()],
        out_specs=vmem(),
        out_shape=jax.ShapeDtypeStruct((tile_rows, rhs, size), f32),
        scratch_shapes=[
            pltpu.VMEM((tile_rows, 2 * rhs, size), bf16),
            pltpu.VMEM((tile_rows + 1, rhs, size), f32),
        ],
        cost_estimate=pl.CostEstimate(flops=3 * split.size * rhs, bytes_accessed=2 * split.size, transcendentals=0),
        compiler_params=pltpu.CompilerParams(vmem_limit_bytes=KERNEL_VMEM),
        name="near",
    )(entries, split, left, right)


def far_rows(tile_rows, halo_tiles, list_ref, split_ref, low_ref, high_ref, parts_ref, rows_ref):
    size = split_ref.shape[1]
    store_parts(parts_ref, 0, low_ref[...], size)
    store_parts(parts_ref, halo_tiles + tile_rows, high_ref[...], size)
    multiply_listed(list_ref, split_ref, parts_ref, rows_ref, 0)


def far_kernel(tile_rows, halo_tiles, list_ref, split_ref, near_ref, low_ref, high_ref, left_ref, right_ref,
               parts_ref, rows_ref):
    size = split_ref.shape[1]
    half = tile_rows // 2
    far_rows(tile_rows, halo_tiles, list_ref, split_ref, low_ref, high_ref, parts_ref, rows_ref)
    for r in range(tile_rows):
        target = left_ref if r < half else right_ref
        at = (r % half) * size
        target[:, at:at + size] = near_ref[r] + rows_ref[r]


def far_scratch(split, rhs, tile_rows, halo_tiles):
    size = split.shape[1]
    return [
        pltpu.VMEM((tile_rows + 2 * halo_tiles, 2 * rhs, size), bf16),
        pltpu.VMEM((tile_rows + 1, rhs, size), f32),
    ]


def far_apply(entries, split, near, low, high, tile_rows, halo_tiles):
    rhs = low.shape[0]
    return pl.pallas_call(
        partial(far_kernel, tile_rows, halo_tiles),
        in_specs=[smem(), vmem(), vmem(), vmem(), vmem()],
        out_specs=[vmem(), vmem()],
        out_shape=[jax.ShapeDtypeStruct(low.shape, f32)] * 2,
        scratch_shapes=far_scratch(split, rhs, tile_rows, halo_tiles),
        cost_estimate=pl.CostEstimate(flops=split.size * rhs, bytes_accessed=split.size, transcendentals=0),
        compiler_params=pltpu.CompilerParams(vmem_limit_bytes=KERNEL_VMEM),
        name="far",
    )(entries, split, near, low, high)


def gram_kernel(tile_rows, halo_tiles, bases, out_rows, list_ref, place_ref, split_ref, near_ref, low_ref, high_ref,
                *refs):
    halves = refs[:2 * bases]
    gram_ref, slice_ref, parts_ref, rows_ref, whole_ref = refs[2 * bases:]
    size = split_ref.shape[1]
    rhs, half = low_ref.shape
    far_rows(tile_rows, halo_tiles, list_ref, split_ref, low_ref, high_ref, parts_ref, rows_ref)
    for i in range(bases):
        whole_ref[i * rhs:(i + 1) * rhs, :half] = halves[2 * i][...]
        whole_ref[i * rhs:(i + 1) * rhs, half:] = halves[2 * i + 1][...]
    for r in range(tile_rows):
        whole_ref[bases * rhs:, r * size:(r + 1) * size] = near_ref[r] + rows_ref[r]
    whole = whole_ref[...]
    gram_ref[...] = lax.dot_general(
        whole, whole, (((1,), (1,)), ((), ())), precision=highest, preferred_element_type=f32
    )
    at = pl.multiple_of(lax.rem(place_ref[0], whole.shape[1] // out_rows) * out_rows, 128)
    slice_ref[...] = whole_ref[:bases * rhs, pl.ds(at, out_rows)]


def gram_apply(entries, place, split, near, low, high, basis, tile_rows, halo_tiles, out_rows):
    rhs = low.shape[0]
    bases = len(basis) // 2
    width = (bases + 1) * rhs
    return pl.pallas_call(
        partial(gram_kernel, tile_rows, halo_tiles, bases, out_rows),
        in_specs=[smem(), smem()] + [vmem()] * (4 + len(basis)),
        out_specs=[vmem(), vmem()],
        out_shape=[
            jax.ShapeDtypeStruct((width, width), f32),
            jax.ShapeDtypeStruct((bases * rhs, out_rows), f32),
        ],
        scratch_shapes=far_scratch(split, rhs, tile_rows, halo_tiles)
        + [pltpu.VMEM((width, 2 * low.shape[1]), f32)],
        cost_estimate=pl.CostEstimate(flops=split.size * rhs, bytes_accessed=split.size, transcendentals=0),
        compiler_params=pltpu.CompilerParams(vmem_limit_bytes=KERNEL_VMEM),
        name="gram",
    )(entries, place, split, near, low, high, *basis)


def swapped(value):
    return pltpu.roll(value, value.shape[-1] // 2, 1)


def scaled(block, real, imaginary):
    return block * real + swapped(block) * imaginary


def stacked(blocks):
    return jnp.concatenate(blocks, axis=0)


def unstacked(value, rhs):
    return [value[i * rhs:(i + 1) * rhs] for i in range(value.shape[0] // rhs)]


def product(left, right):
    return jnp.dot(left, right, precision=highest, preferred_element_type=f32)


def solve_group(gram, zr, zi, rhs):
    lanes = 2 * GROUP * rhs
    half = lanes // 2
    lane = lax.broadcasted_iota(jnp.int32, (rhs, lanes), 1)
    line = lax.broadcasted_iota(jnp.int32, (rhs, lanes), 0)
    front = lane < half
    sign = jnp.where(lane[:1] < half, -1.0, 1.0).astype(f32)
    eye = (lane % rhs == line).astype(f32)
    tall_line = lax.broadcasted_iota(jnp.int32, (lanes, lanes), 0)
    tall_lane = lax.broadcasted_iota(jnp.int32, (lanes, lanes), 1)
    same_point = (tall_line % half) // rhs == (tall_lane % half) // rhs
    sums = same_point.astype(f32)

    def right_factor(block):
        turned = swapped(block) * sign
        return jnp.where(same_point, stacked([block] * GROUP + [turned] * GROUP), 0.0)

    def operator(blocks):
        out = [scaled(b, zr, zi) for b in blocks] + [jnp.zeros_like(blocks[0])]
        for i, b in enumerate(blocks):
            out[i + 1] = out[i + 1] - b
        return out

    def inverse(system):
        real = jnp.where(front, system, eye)
        imaginary = jnp.where(front, swapped(system), 0.0)
        origin = (lane % half) // rhs * rhs
        for p in range(rhs):
            column_r = jnp.take_along_axis(real, origin + p, axis=1)
            column_i = jnp.take_along_axis(imaginary, origin + p, axis=1)
            pivot_r, pivot_i = column_r[p:p + 1], column_i[p:p + 1]
            scale = 1.0 / (pivot_r * pivot_r + pivot_i * pivot_i)
            inverse_r, inverse_i = pivot_r * scale, -pivot_i * scale
            row_r, row_i = real[p:p + 1], imaginary[p:p + 1]
            lead_r = row_r * inverse_r - row_i * inverse_i
            lead_i = row_r * inverse_i + row_i * inverse_r
            here = line == p
            real = jnp.where(here, lead_r, real - (column_r * lead_r - column_i * lead_i))
            imaginary = jnp.where(here, lead_i, imaginary - (column_r * lead_i + column_i * lead_r))
        return jnp.where(front, swapped(real), imaginary)

    shadow = gram[:rhs]
    identity = jnp.where(front, eye, 0.0)
    direction, residual, result = [identity], [identity], []
    for iteration in range(ITERS):
        image = operator(direction)
        tall = stacked(image)
        image_gram = product(shadow[:, :tall.shape[0]], tall)
        tall_residual = stacked(residual)
        residual_gram = product(shadow[:, :tall_residual.shape[0]], tall_residual)
        solver = inverse(image_gram)
        alpha = right_factor(product(solver, right_factor(residual_gram)))
        moved = unstacked(product(stacked(image + direction), alpha), rhs)
        moved_image, moved_direction = moved[:len(image)], moved[len(image):]
        partial_block = [-m for m in moved_image]
        for i, r in enumerate(residual):
            partial_block[i] = partial_block[i] + r
        second = operator(partial_block)
        tall_second = stacked(second)
        tall_partial = stacked(partial_block + [jnp.zeros_like(identity)])
        depth = tall_second.shape[0]
        weighted = product(gram[:depth, :depth], tall_second)
        turned = swapped(weighted) * -sign
        lines = [
            jnp.sum(tall_second * weighted, axis=0, keepdims=True),
            jnp.sum(tall_partial * weighted, axis=0, keepdims=True),
            jnp.sum(tall_partial * turned, axis=0, keepdims=True),
        ]
        spread = product(stacked(lines + [jnp.zeros((5, lanes), f32)]), sums)
        inverse_norm = 1.0 / spread[0:1]
        omega_r = spread[1:2] * inverse_norm
        omega_i = -spread[2:3] * inverse_norm * sign
        step = [scaled(b, omega_r, omega_i) for b in partial_block]
        for i, m in enumerate(moved_direction):
            step[i] = step[i] + m
        for i, r in enumerate(result):
            step[i] = step[i] + r
        result = step
        if iteration + 1 < ITERS:
            residual = [-scaled(b, omega_r, omega_i) for b in second]
            for i, s in enumerate(partial_block):
                residual[i] = residual[i] + s
            beta = -product(solver, right_factor(weighted[:rhs]))
            base = [-scaled(b, omega_r, omega_i) for b in image]
            for i, d in enumerate(direction):
                base[i] = base[i] + d
            turned_base = unstacked(product(stacked(base), right_factor(beta)), rhs)
            direction = list(residual)
            for i, b in enumerate(turned_base):
                direction[i] = direction[i] + b
    return stacked(result)


def finish_kernel(rhs, groups, grams, *refs):
    gram_refs, (points_ref, table_ref, slice_ref, out_ref) = refs[:grams], refs[grams:]
    gram = gram_refs[0][...]
    for ref in gram_refs[1:]:
        gram = gram + ref[...]
    lanes = 2 * GROUP * rhs
    weights = None
    for g in range(groups):
        solved = solve_group(gram, points_ref[2 * g:2 * g + 1], points_ref[2 * g + 1:2 * g + 2], rhs)
        term = product(solved, table_ref[g * lanes:(g + 1) * lanes])
        weights = term if weights is None else weights + term
    out_ref[...] = lax.dot_general(
        slice_ref[...], weights, (((0,), (0,)), ((), ())), precision=highest, preferred_element_type=f32
    )


def contour_tables(point_count, rhs):
    groups = -(-point_count // GROUP)
    points = np.zeros((-(-2 * groups // 8) * 8, 2 * GROUP * rhs), np.float32)
    table = np.zeros((groups, 2, GROUP, rhs, 2, MOM, rhs), np.float32)
    factor = contour_radius / point_count
    powers = np.arange(1, MOM + 1)
    for j in range(groups * GROUP):
        g, slot = divmod(j, GROUP)
        angle = np.pi * (2 * min(j, point_count - 1) + 1) / point_count
        lanes = np.arange(slot * rhs, (slot + 1) * rhs)
        points[2 * g, lanes] = points[2 * g, GROUP * rhs + lanes] = contour_radius * np.cos(angle) - SHIFT
        imaginary = contour_center + contour_radius * np.sin(angle)
        points[2 * g + 1, lanes] = -imaginary
        points[2 * g + 1, GROUP * rhs + lanes] = imaginary
        if j >= point_count:
            continue
        cosine, sine = factor * np.cos(powers * angle), factor * np.sin(powers * angle)
        for c in range(rhs):
            table[g, 0, slot, c, 0, :, c] = cosine
            table[g, 0, slot, c, 1, :, c] = sine
            table[g, 1, slot, c, 0, :, c] = -sine
            table[g, 1, slot, c, 1, :, c] = cosine
    return groups, points, table.reshape(groups * 2 * GROUP * rhs, 2 * MOM * rhs)


def finish(grams, basis_slice, point_count, rhs):
    groups, points, table = contour_tables(point_count, rhs)
    return pl.pallas_call(
        partial(finish_kernel, rhs, groups, len(grams)),
        in_specs=[vmem()] * (len(grams) + 3),
        out_specs=vmem(),
        out_shape=jax.ShapeDtypeStruct((basis_slice.shape[1], table.shape[1]), f32),
        compiler_params=pltpu.CompilerParams(vmem_limit_bytes=KERNEL_VMEM),
        name="finish",
    )(*grams, jnp.asarray(points), jnp.asarray(table), basis_slice)


def body(right_sides, jacobian_tiles, row_starts, tile_columns):
    tile_rows = row_starts.shape[0]
    rhs = right_sides.shape[0]
    halo_tiles = tile_rows // 2
    half = right_sides.shape[1] // 2
    count = lax.axis_size("rows")
    quad_count = lax.axis_size("quad")
    forward = [(i, (i + 1) % count) for i in range(count)]
    backward = [(target, source) for source, target in forward]
    place = (lax.axis_index("rows") * quad_count + lax.axis_index("quad")).reshape(1)
    out_rows = right_sides.shape[1] // quad_count

    left, right = right_sides[:, :half], right_sides[:, half:]
    low = lax.ppermute(right, "rows", forward)
    high = lax.ppermute(left, "rows", backward)
    split, near_list, far_list, near = first_apply(
        jacobian_tiles, row_starts, tile_columns, place, left, right, quad_count, tile_rows, halo_tiles
    )
    basis = []
    for power in range(DEGREE):
        if power > 0:
            low = lax.ppermute(right, "rows", forward)
            high = lax.ppermute(left, "rows", backward)
            near = near_apply(near_list, split, left, right, tile_rows, halo_tiles)
        basis += [left, right]
        if power + 1 < DEGREE:
            left, right = far_apply(far_list, split, near, low, high, tile_rows, halo_tiles)
    gram, basis_slice = gram_apply(
        far_list, place, split, near, low, high, basis, tile_rows, halo_tiles, out_rows
    )
    distance = 1
    while distance * 4 < count:
        gram = gram + lax.ppermute(gram, "rows", [(i, i ^ distance) for i in range(count)])
        distance *= 2
    grams = [gram] + [
        lax.ppermute(gram, "rows", [(i, i ^ (distance * k)) for i in range(count)])
        for k in range(1, count // distance)
    ]
    result = finish(grams, basis_slice, quad_count, rhs)
    return result.reshape(1, 1, result.shape[0], result.shape[1])


def solution(mesh):
    in_specs = (P(None, "rows"), P("rows", None, None), P("rows"), P("rows"))
    out_specs = P("rows", "quad", None, None)
    return jax.shard_map(body, mesh=mesh, in_specs=in_specs, out_specs=out_specs, check_vma=False)
```

```python
from functools import partial

import jax
import jax.numpy as jnp
import numpy as np
from jax import lax
from jax.experimental import pallas as pl
from jax.experimental.pallas import tpu as pltpu
from jax.sharding import PartitionSpec as P

MOM = 8
ITERS = 2
DEGREE = 2 * ITERS

contour_center = 3.0
contour_radius = 2.0
SHIFT = -7.0
SCALE = 1024.0
NEAR_CHUNK = 32
FAR_CHUNK = 48
SPLIT_STEP = 32
KERNEL_VMEM = 16 << 20
PIVOTS = 8
GROUP = 4
highest = lax.Precision.HIGHEST
f32 = jnp.float32
bf16 = jnp.bfloat16


def vmem():
    return pl.BlockSpec(memory_space=pltpu.VMEM)


def smem():
    return pl.BlockSpec(memory_space=pltpu.SMEM)


def split_parts(value):
    high = value.astype(bf16)
    return high, (value - high.astype(f32)).astype(bf16)


def first_kernel(tile_rows, halo_tiles, quad_count, place_ref, starts_hbm, columns_hbm, tiles_hbm, block_ref,
                 split_ref, near_ref, far_ref, out_ref, tiles_ref, parts_ref, rows_ref, starts_ref, columns_ref,
                 tile_sems, index_sems):
    count, size = tiles_ref.shape[0], tiles_ref.shape[1]
    rhs = block_ref.shape[0]
    starts_copy = pltpu.make_async_copy(starts_hbm, starts_ref, index_sems.at[0])
    columns_copy = pltpu.make_async_copy(columns_hbm, columns_ref, index_sems.at[1])
    starts_copy.start()
    columns_copy.start()

    def tiles_copy(step):
        span = pl.ds(step * SPLIT_STEP, SPLIT_STEP)
        return pltpu.make_async_copy(tiles_hbm.at[span], tiles_ref.at[span], tile_sems.at[step])

    for step in range(count // SPLIT_STEP):
        tiles_copy(step).start()
    store_parts(parts_ref, 0, block_ref[...], size)
    starts_copy.wait()
    columns_copy.wait()
    origin = lax.div(place_ref[0], quad_count) * tile_rows - halo_tiles
    base = starts_ref[0]

    def chunk(step, carry):
        row, near, far, total = carry
        tiles_copy(step).wait()
        for u in range(SPLIT_STEP):
            t = step * SPLIT_STEP + u
            following = starts_ref[jnp.minimum(row + 1, tile_rows - 1)] - base
            fresh = (row + 1 < tile_rows) & (t >= following)
            row = row + fresh.astype(jnp.int32)
            column = columns_ref[t] - origin
            inside = (column >= halo_tiles) & (column < halo_tiles + tile_rows)
            entry = (t * 64 + column) * 32 + row
            near_ref[1 + near] = entry
            far_ref[1 + far] = entry
            counted = inside.astype(jnp.int32)
            near = near + counted
            far = far + (1 - counted)
            high, low = split_parts(tiles_ref[t])
            high, low = high.T, low.T
            split_ref[t, :, :size] = high
            split_ref[t, :, size:] = low
            local = jnp.clip(column - halo_tiles, 0, tile_rows - 1)
            both = jnp.dot(parts_ref[local], jnp.concatenate([high, low], axis=1), preferred_element_type=f32)
            term = (both[:rhs, :size] + both[rhs:, :size]) + (both[:rhs, size:] + both[rhs:, size:])
            zero = jnp.zeros_like(total)
            total = jnp.where(fresh, zero, total) + jnp.where(inside, term, zero)
            rows_ref[row] = total
        return row, near, far, total

    zero = jnp.int32(0)
    _, near, far, _ = lax.fori_loop(
        0, count // SPLIT_STEP, chunk, (zero, zero, zero, jnp.zeros((rhs, size), f32))
    )
    near_ref[0] = near
    far_ref[0] = far
    padding = halo_tiles * 32 + tile_rows
    for u in range(NEAR_CHUNK):
        near_ref[1 + near + u] = padding
    for u in range(FAR_CHUNK):
        far_ref[1 + far + u] = padding
    shifted_rows(rows_ref, [block_ref], out_ref, tile_rows)


def shifted_rows(rows_ref, block_refs, out_ref, tile_rows):
    per_ref = tile_rows // len(block_refs)
    size = rows_ref.shape[2]
    for r in range(tile_rows):
        source = block_refs[r // per_ref]
        at = (r % per_ref) * size
        out_ref[r] = (rows_ref[r] - SHIFT * source[:, at:at + size]) * (1.0 / SCALE)


def first_apply(tiles, row_starts, tile_columns, place, block, quad_count, tile_rows, halo_tiles):
    count, size = tiles.shape[0], tiles.shape[1]
    rhs = block.shape[0]
    hbm = pl.BlockSpec(memory_space=pl.ANY)
    return pl.pallas_call(
        partial(first_kernel, tile_rows, halo_tiles, quad_count),
        in_specs=[smem(), hbm, hbm, hbm, vmem()],
        out_specs=[vmem(), smem(), smem(), vmem()],
        out_shape=[
            jax.ShapeDtypeStruct((count, size, 2 * size), bf16),
            jax.ShapeDtypeStruct((1 + count + NEAR_CHUNK,), jnp.int32),
            jax.ShapeDtypeStruct((1 + count + FAR_CHUNK,), jnp.int32),
            jax.ShapeDtypeStruct((tile_rows, rhs, size), f32),
        ],
        scratch_shapes=[
            pltpu.VMEM((count, size, size), f32),
            pltpu.VMEM((tile_rows, 2 * rhs, size), bf16),
            pltpu.VMEM((tile_rows, rhs, size), f32),
            pltpu.SMEM((tile_rows,), jnp.int32),
            pltpu.SMEM((count,), jnp.int32),
            pltpu.SemaphoreType.DMA((count // SPLIT_STEP,)),
            pltpu.SemaphoreType.DMA((2,)),
        ],
        cost_estimate=pl.CostEstimate(flops=8 * tiles.size * rhs, bytes_accessed=8 * tiles.size, transcendentals=0),
        compiler_params=pltpu.CompilerParams(vmem_limit_bytes=24 << 20),
        name="first",
    )(
        place,
        pltpu.with_memory_space_constraint(row_starts, pltpu.HBM),
        pltpu.with_memory_space_constraint(tile_columns, pltpu.HBM),
        pltpu.with_memory_space_constraint(tiles, pltpu.HBM),
        block,
    )


def multiply_listed(per_step, list_ref, split_ref, parts_ref, rows_ref, first_block):
    rhs, size = rows_ref.shape[1:]
    rows_ref[...] = jnp.zeros_like(rows_ref)
    count = list_ref[0]

    def chunk(index, carry):
        total, last = carry
        products, owners = [], []
        for u in range(per_step):
            entry = list_ref[1 + index * per_step + u]
            row = entry & 31
            column = (entry >> 5) & 63
            tile = entry >> 11
            both = jnp.dot(parts_ref[column - first_block], split_ref[tile], preferred_element_type=f32)
            products.append((both[:rhs, :size] + both[rhs:, :size]) + (both[:rhs, size:] + both[rhs:, size:]))
            owners.append(row)
        for product, row in zip(products, owners):
            total = jnp.where(row == last, total, jnp.zeros_like(total)) + product
            rows_ref[row] = total
            last = row
        return total, last

    steps = lax.div(count + (per_step - 1), per_step)
    lax.fori_loop(0, steps, chunk, (jnp.zeros((rhs, size), f32), jnp.int32(-1)))


def store_parts(parts_ref, first, value, size):
    rhs = value.shape[0]
    high, low = split_parts(value)
    for b in range(value.shape[1] // size):
        parts_ref[first + b, :rhs, :] = high[:, b * size:(b + 1) * size]
        parts_ref[first + b, rhs:, :] = low[:, b * size:(b + 1) * size]


def near_kernel(tile_rows, halo_tiles, list_ref, split_ref, left_ref, right_ref, out_ref, parts_ref, rows_ref):
    size = split_ref.shape[1]
    half = tile_rows // 2
    store_parts(parts_ref, 0, left_ref[...], size)
    store_parts(parts_ref, half, right_ref[...], size)
    multiply_listed(NEAR_CHUNK, list_ref, split_ref, parts_ref, rows_ref, halo_tiles)
    shifted_rows(rows_ref, [left_ref, right_ref], out_ref, tile_rows)


def near_apply(entries, split, left, right, tile_rows, halo_tiles):
    rhs = left.shape[0]
    size = split.shape[1]
    return pl.pallas_call(
        partial(near_kernel, tile_rows, halo_tiles),
        in_specs=[smem(), vmem(), vmem(), vmem()],
        out_specs=vmem(),
        out_shape=jax.ShapeDtypeStruct((tile_rows, rhs, size), f32),
        scratch_shapes=[
            pltpu.VMEM((tile_rows, 2 * rhs, size), bf16),
            pltpu.VMEM((tile_rows + 1, rhs, size), f32),
        ],
        cost_estimate=pl.CostEstimate(flops=3 * split.size * rhs, bytes_accessed=2 * split.size, transcendentals=0),
        compiler_params=pltpu.CompilerParams(vmem_limit_bytes=KERNEL_VMEM),
        name="near",
    )(entries, split, left, right)


def far_rows(tile_rows, halo_tiles, list_ref, split_ref, low_ref, high_ref, parts_ref, rows_ref):
    size = split_ref.shape[1]
    width = halo_tiles * size
    store_parts(parts_ref, 0, low_ref[:, low_ref.shape[1] - width:], size)
    store_parts(parts_ref, halo_tiles + tile_rows, high_ref[:, :width], size)
    multiply_listed(FAR_CHUNK, list_ref, split_ref, parts_ref, rows_ref, 0)


def far_kernel(tile_rows, halo_tiles, list_ref, split_ref, near_ref, low_ref, high_ref, left_ref, right_ref,
               parts_ref, rows_ref):
    size = split_ref.shape[1]
    half = tile_rows // 2
    far_rows(tile_rows, halo_tiles, list_ref, split_ref, low_ref, high_ref, parts_ref, rows_ref)
    for r in range(tile_rows):
        target = left_ref if r < half else right_ref
        at = (r % half) * size
        target[:, at:at + size] = near_ref[r] + rows_ref[r] * (1.0 / SCALE)


def far_scratch(split, rhs, tile_rows, halo_tiles):
    size = split.shape[1]
    return [
        pltpu.VMEM((tile_rows + 2 * halo_tiles, 2 * rhs, size), bf16),
        pltpu.VMEM((tile_rows + 1, rhs, size), f32),
    ]


def far_apply(entries, split, near, low, high, tile_rows, halo_tiles):
    rhs = low.shape[0]
    return pl.pallas_call(
        partial(far_kernel, tile_rows, halo_tiles),
        in_specs=[smem(), vmem(), vmem(), vmem(), vmem()],
        out_specs=[vmem(), vmem()],
        out_shape=[jax.ShapeDtypeStruct((rhs, tile_rows // 2 * split.shape[1]), f32)] * 2,
        scratch_shapes=far_scratch(split, rhs, tile_rows, halo_tiles),
        cost_estimate=pl.CostEstimate(flops=split.size * rhs, bytes_accessed=split.size, transcendentals=0),
        compiler_params=pltpu.CompilerParams(vmem_limit_bytes=KERNEL_VMEM),
        name="far",
    )(entries, split, near, low, high)


def gram_kernel(tile_rows, halo_tiles, bases, out_rows, list_ref, place_ref, split_ref, near_ref, low_ref, high_ref,
                *refs):
    pieces = refs[:2 * bases - 1]
    gram_ref, slice_ref, parts_ref, rows_ref, whole_ref = refs[2 * bases - 1:]
    size = split_ref.shape[1]
    rhs = low_ref.shape[0]
    half = whole_ref.shape[1] // 2
    far_rows(tile_rows, halo_tiles, list_ref, split_ref, low_ref, high_ref, parts_ref, rows_ref)
    whole_ref[:rhs, :] = pieces[0][...]
    for i in range(1, bases):
        whole_ref[i * rhs:(i + 1) * rhs, :half] = pieces[2 * i - 1][...]
        whole_ref[i * rhs:(i + 1) * rhs, half:] = pieces[2 * i][...]
    for r in range(tile_rows):
        whole_ref[bases * rhs:, r * size:(r + 1) * size] = near_ref[r] + rows_ref[r] * (1.0 / SCALE)
    whole = whole_ref[...]
    gram_ref[...] = lax.dot_general(
        whole, whole, (((1,), (1,)), ((), ())), precision=highest, preferred_element_type=f32
    )
    at = pl.multiple_of(lax.rem(place_ref[0], whole.shape[1] // out_rows) * out_rows, 128)
    slice_ref[...] = whole_ref[:bases * rhs, pl.ds(at, out_rows)]


def gram_apply(entries, place, split, near, low, high, basis, tile_rows, halo_tiles, out_rows):
    rhs = low.shape[0]
    bases = (len(basis) + 1) // 2
    width = (bases + 1) * rhs
    return pl.pallas_call(
        partial(gram_kernel, tile_rows, halo_tiles, bases, out_rows),
        in_specs=[smem(), smem()] + [vmem()] * (4 + len(basis)),
        out_specs=[vmem(), vmem()],
        out_shape=[
            jax.ShapeDtypeStruct((width, width), f32),
            jax.ShapeDtypeStruct((bases * rhs, out_rows), f32),
        ],
        scratch_shapes=far_scratch(split, rhs, tile_rows, halo_tiles)
        + [pltpu.VMEM((width, basis[0].shape[1]), f32)],
        cost_estimate=pl.CostEstimate(flops=split.size * rhs, bytes_accessed=split.size, transcendentals=0),
        compiler_params=pltpu.CompilerParams(vmem_limit_bytes=KERNEL_VMEM),
        name="gram",
    )(entries, place, split, near, low, high, *basis)


def swapped(value):
    return pltpu.roll(value, value.shape[-1] // 2, 1)


def scaled(block, real, imaginary):
    return block * real + swapped(block) * imaginary


def stacked(blocks):
    return jnp.concatenate(blocks, axis=0)


def unstacked(value, rhs):
    return [value[i * rhs:(i + 1) * rhs] for i in range(value.shape[0] // rhs)]


def product(left, right):
    return jnp.dot(left, right, precision=highest, preferred_element_type=f32)


def solve_group(gram, zr, zi, rhs):
    lanes = 2 * GROUP * rhs
    half = lanes // 2
    lane = lax.broadcasted_iota(jnp.int32, (rhs, lanes), 1)
    line = lax.broadcasted_iota(jnp.int32, (rhs, lanes), 0)
    front = lane < half
    sign = jnp.where(lane[:1] < half, -1.0, 1.0).astype(f32)
    eye = (lane % rhs == line).astype(f32)
    tall_line = lax.broadcasted_iota(jnp.int32, (lanes, lanes), 0)
    tall_lane = lax.broadcasted_iota(jnp.int32, (lanes, lanes), 1)
    same_point = (tall_line % half) // rhs == (tall_lane % half) // rhs
    sums = same_point.astype(f32)

    def right_factor(block):
        turned = swapped(block) * sign
        return jnp.where(same_point, stacked([block] * GROUP + [turned] * GROUP), 0.0)

    def operator(blocks):
        out = [scaled(b, zr, zi) for b in blocks] + [jnp.zeros_like(blocks[0])]
        for i, b in enumerate(blocks):
            out[i + 1] = out[i + 1] - SCALE * b
        return out

    def eliminate(system, known, with_inverse):
        work = [(jnp.where(front, system, swapped(known)), jnp.where(front, swapped(system), known))]
        if with_inverse:
            work.append((eye, jnp.zeros_like(eye)))
        origin = (lane % half) // rhs * rhs
        for start in range(0, rhs, PIVOTS):
            columns = [
                tuple(jnp.take_along_axis(part, origin + p, axis=1) for part in work[0])
                for p in range(start, start + PIVOTS)
            ]
            for p in range(start, start + PIVOTS):
                here = line == p
                column_r, column_i = columns[p - start]
                pivot_r, pivot_i = column_r[p:p + 1], column_i[p:p + 1]
                scale = 1.0 / (pivot_r * pivot_r + pivot_i * pivot_i)
                inverse_r, inverse_i = pivot_r * scale, -pivot_i * scale

                def reduced(pair):
                    real, imaginary = pair
                    row_r, row_i = real[p:p + 1], imaginary[p:p + 1]
                    lead_r = row_r * inverse_r - row_i * inverse_i
                    lead_i = row_r * inverse_i + row_i * inverse_r
                    return (
                        jnp.where(here, lead_r, real - (column_r * lead_r - column_i * lead_i)),
                        jnp.where(here, lead_i, imaginary - (column_r * lead_i + column_i * lead_r)),
                    )

                for k in range(p - start + 1, PIVOTS):
                    columns[k] = reduced(columns[k])
                work = [reduced(pair) for pair in work]
        solved = jnp.where(front, swapped(work[0][0]), work[0][1])
        if not with_inverse:
            return solved, None
        return solved, jnp.where(front, work[1][0], swapped(work[1][1]))

    shadow = gram[:rhs]
    identity = jnp.where(front, eye, 0.0)
    direction, residual, result = [identity], [identity], []
    for iteration in range(ITERS):
        image = operator(direction)
        tall = stacked(image)
        image_gram = product(shadow[:, :tall.shape[0]], tall)
        tall_residual = stacked(residual)
        residual_gram = product(shadow[:, :tall_residual.shape[0]], tall_residual)
        alpha, solver = eliminate(image_gram, residual_gram, iteration + 1 < ITERS)
        alpha = right_factor(alpha)
        moved = unstacked(product(stacked(image + direction), alpha), rhs)
        moved_image, moved_direction = moved[:len(image)], moved[len(image):]
        partial_block = [-m for m in moved_image]
        for i, r in enumerate(residual):
            partial_block[i] = partial_block[i] + r
        second = operator(partial_block)
        tall_second = stacked(second)
        tall_partial = stacked(partial_block + [jnp.zeros_like(identity)])
        depth = tall_second.shape[0]
        weighted = product(gram[:depth, :depth], tall_second)
        turned = swapped(weighted) * -sign
        lines = [
            jnp.sum(tall_second * weighted, axis=0, keepdims=True),
            jnp.sum(tall_partial * weighted, axis=0, keepdims=True),
            jnp.sum(tall_partial * turned, axis=0, keepdims=True),
        ]
        spread = product(stacked(lines + [jnp.zeros((5, lanes), f32)]), sums)
        inverse_norm = 1.0 / spread[0:1]
        omega_r = spread[1:2] * inverse_norm
        omega_i = -spread[2:3] * inverse_norm * sign
        step = [scaled(b, omega_r, omega_i) for b in partial_block]
        for i, m in enumerate(moved_direction):
            step[i] = step[i] + m
        for i, r in enumerate(result):
            step[i] = step[i] + r
        result = step
        if iteration + 1 < ITERS:
            residual = [-scaled(b, omega_r, omega_i) for b in second]
            for i, s in enumerate(partial_block):
                residual[i] = residual[i] + s
            beta = -product(solver, right_factor(weighted[:rhs]))
            base = [-scaled(b, omega_r, omega_i) for b in image]
            for i, d in enumerate(direction):
                base[i] = base[i] + d
            turned_base = unstacked(product(stacked(base), right_factor(beta)), rhs)
            direction = list(residual)
            for i, b in enumerate(turned_base):
                direction[i] = direction[i] + b
    return stacked(result)


def finish_kernel(rhs, groups, grams, *refs):
    gram_refs, (points_ref, table_ref, slice_ref, out_ref) = refs[:grams], refs[grams:]
    gram = gram_refs[0][...]
    for ref in gram_refs[1:]:
        gram = gram + ref[...]
    lanes = 2 * GROUP * rhs
    weights = None
    for g in range(groups):
        solved = solve_group(gram, points_ref[2 * g:2 * g + 1], points_ref[2 * g + 1:2 * g + 2], rhs)
        term = product(solved, table_ref[g * lanes:(g + 1) * lanes])
        weights = term if weights is None else weights + term
    out_ref[...] = lax.dot_general(
        slice_ref[...], weights, (((0,), (0,)), ((), ())), precision=highest, preferred_element_type=f32
    )


def contour_tables(point_count, rhs):
    groups = -(-point_count // GROUP)
    points = np.zeros((-(-2 * groups // 8) * 8, 2 * GROUP * rhs), np.float32)
    table = np.zeros((groups, 2, GROUP, rhs, 2, MOM, rhs), np.float32)
    factor = contour_radius / point_count
    powers = np.arange(1, MOM + 1)
    for j in range(groups * GROUP):
        g, slot = divmod(j, GROUP)
        angle = np.pi * (2 * min(j, point_count - 1) + 1) / point_count
        lanes = np.arange(slot * rhs, (slot + 1) * rhs)
        points[2 * g, lanes] = points[2 * g, GROUP * rhs + lanes] = contour_radius * np.cos(angle) - SHIFT
        imaginary = contour_center + contour_radius * np.sin(angle)
        points[2 * g + 1, lanes] = -imaginary
        points[2 * g + 1, GROUP * rhs + lanes] = imaginary
        if j >= point_count:
            continue
        cosine, sine = factor * np.cos(powers * angle), factor * np.sin(powers * angle)
        for c in range(rhs):
            table[g, 0, slot, c, 0, :, c] = cosine
            table[g, 0, slot, c, 1, :, c] = sine
            table[g, 1, slot, c, 0, :, c] = -sine
            table[g, 1, slot, c, 1, :, c] = cosine
    return groups, points, table.reshape(groups * 2 * GROUP * rhs, 2 * MOM * rhs)


def finish(grams, basis_slice, point_count, rhs):
    groups, points, table = contour_tables(point_count, rhs)
    return pl.pallas_call(
        partial(finish_kernel, rhs, groups, len(grams)),
        in_specs=[vmem()] * (len(grams) + 3),
        out_specs=vmem(),
        out_shape=jax.ShapeDtypeStruct((basis_slice.shape[1], table.shape[1]), f32),
        compiler_params=pltpu.CompilerParams(vmem_limit_bytes=KERNEL_VMEM),
        name="finish",
    )(*grams, jnp.asarray(points), jnp.asarray(table), basis_slice)


def body(right_sides, jacobian_tiles, row_starts, tile_columns):
    tile_rows = row_starts.shape[0]
    rhs = right_sides.shape[0]
    halo_tiles = tile_rows // 2
    count = lax.axis_size("rows")
    quad_count = lax.axis_size("quad")
    forward = [(i, (i + 1) % count) for i in range(count)]
    backward = [(target, source) for source, target in forward]
    place = (lax.axis_index("rows") * quad_count + lax.axis_index("quad")).reshape(1)
    out_rows = right_sides.shape[1] // quad_count

    low = lax.ppermute(right_sides, "rows", forward)
    high = lax.ppermute(right_sides, "rows", backward)
    split, near_list, far_list, near = first_apply(
        jacobian_tiles, row_starts, tile_columns, place, right_sides, quad_count, tile_rows, halo_tiles
    )
    basis = [right_sides]
    for power in range(DEGREE):
        if power > 0:
            low = lax.ppermute(right, "rows", forward)
            high = lax.ppermute(left, "rows", backward)
            near = near_apply(near_list, split, left, right, tile_rows, halo_tiles)
            basis += [left, right]
        if power + 1 < DEGREE:
            left, right = far_apply(far_list, split, near, low, high, tile_rows, halo_tiles)
    gram, basis_slice = gram_apply(
        far_list, place, split, near, low, high, basis, tile_rows, halo_tiles, out_rows
    )
    distance = 1
    while distance * 4 < count:
        gram = gram + lax.ppermute(gram, "rows", [(i, i ^ distance) for i in range(count)])
        distance *= 2
    grams = [gram] + [
        lax.ppermute(gram, "rows", [(i, i ^ (distance * k)) for i in range(count)])
        for k in range(1, count // distance)
    ]
    result = finish(grams, basis_slice, quad_count, rhs)
    return result.reshape(1, 1, result.shape[0], result.shape[1])


def solution(mesh):
    in_specs = (P(None, "rows"), P("rows", None, None), P("rows"), P("rows"))
    out_specs = P("rows", "quad", None, None)
    return jax.shard_map(body, mesh=mesh, in_specs=in_specs, out_specs=out_specs, check_vma=False)
```
